32 devices in a mesh: seq: 16 (over z, y, x), head: 2 (over core).
Axes of the slice: x: 2, y: 2, z: 4, core: 2. Of those that a mesh axis runs over, the one named last changes fastest.
Arguments:
- queries: bfloat16 [4096, 2048], P('seq', 'head'), may hold values from -12 to 12
- key_vectors: bfloat16 [4096, 2048], P('seq', 'head'), may hold values from -12 to 12
- value_vectors: bfloat16 [4096, 2048], P('seq', 'head'), may hold values from -32 to 32
- gain_query: float32 [128], replicated, may hold values from 0.1 to 1.9
- gain_key: float32 [128], replicated, may hold values from 0.1 to 1.9
- grad_out: bfloat16 [4096, 2048], P('seq', 'head'), may hold values from -24 to 24
Outputs:
- attended: bfloat16 [4096, 2048], P('seq', 'head')
- grad_query: bfloat16 [4096, 2048], P('seq', 'head')
- grad_key: bfloat16 [4096, 2048], P('seq', 'head')
- grad_value: bfloat16 [4096, 2048], P('seq', 'head')
- gain_grads: float32 [2, 128], replicated
The draws below stay inside these ranges and needn't reach their ends.
All inputs are finite; a program needn't handle non-finite values.
Results may differ from the reference program's by a relative error of at most 0.039.
Values may be sent and summed in bfloat16 or wider, within the bound.
A program may use at most 128 MiB of HBM per device.

```python
import math
from functools import partial
import jax
import jax.numpy as jnp
from jax import lax

HEADS = 16
DH = 128
BLOCK = 256
TOKENS = 4096
LEVELS = 4


def multiscale(base_key, row_count, feature_width, amplitude):
    scale_count = (row_count // BLOCK).bit_length()
    running = jnp.zeros((row_count, feature_width), jnp.float32)
    for scale_index in range(scale_count):
        groups = row_count // (BLOCK << scale_index)
        component = jax.random.normal(jax.random.fold_in(base_key, 100 + scale_index), (groups, 1, feature_width), jnp.float32)
        running = (running.reshape(groups, row_count // groups, feature_width) + component).reshape(row_count, feature_width)
    return amplitude * running


def pooled_runs(base_key, run_amplitude):
    run_count = TOKENS // 8
    pool_count = BLOCK // 2
    pool_vectors = jax.random.normal(jax.random.fold_in(base_key, 29), (pool_count, HEADS, DH), jnp.float32)
    selected = jax.random.randint(jax.random.fold_in(base_key, 31), (run_count, HEADS), 0, pool_count)
    head_index = jnp.arange(HEADS, dtype=jnp.int32)[None, :]
    picked = pool_vectors[selected, head_index]
    return run_amplitude * jnp.repeat(picked.reshape(run_count, HEADS * DH), 8, axis=0)


def own_noise(base_key, dims_out):
    return jax.random.normal(base_key, dims_out, jnp.float32)


def query_key_draw(key, salt):
    amplitude = 0.3
    run_amplitude = 2.0
    feature_width = HEADS * DH
    shared = multiscale(jax.random.fold_in(key, 7), TOKENS, feature_width, amplitude)
    runs_part = pooled_runs(key, run_amplitude)
    noise_part = own_noise(jax.random.fold_in(key, salt), (TOKENS, feature_width))
    return jnp.clip(noise_part + shared + runs_part, -12.0, 12.0).astype(jnp.bfloat16)


def draw_queries(key, part):
    return query_key_draw(key, 11)


def draw_key_vectors(key, part):
    return query_key_draw(key, 13)


def draw_value_vectors(key, part):
    feature_width = HEADS * DH
    run_count = TOKENS // 8
    shared = multiscale(jax.random.fold_in(key, 17), TOKENS, feature_width, 0.5)
    run_vectors = jax.random.normal(jax.random.fold_in(key, 37), (run_count, feature_width), jnp.float32)
    runs_part = 1.5 * jnp.repeat(run_vectors, 8, axis=0)
    noise_part = own_noise(jax.random.fold_in(key, 19), (TOKENS, feature_width))
    return jnp.clip(noise_part + shared + runs_part, -32.0, 32.0).astype(jnp.bfloat16)


def draw_grad_out(key, part):
    feature_width = HEADS * DH
    positions = jnp.arange(TOKENS, dtype=jnp.int32).astype(jnp.float32)[:, None] / TOKENS
    rising = 1.0 + 2.0 * positions
    noise_part = own_noise(jax.random.fold_in(key, 23), (TOKENS, feature_width))
    return jnp.clip(rising * noise_part, -24.0, 24.0).astype(jnp.bfloat16)


def setup_inputs(seed: int = 0) -> dict:
    key_of = jax.random.split(jax.random.key(seed), 7)
    queries = draw_queries(jax.random.fold_in(key_of[6], 71), 0)
    key_vectors = draw_key_vectors(jax.random.fold_in(key_of[6], 71), 0)
    value_vectors = draw_value_vectors(jax.random.fold_in(key_of[6], 71), 0)
    gain_query = jnp.clip(1.0 + 0.18 * jax.random.normal(key_of[3], (DH,), jnp.float32), 0.1, 1.9)
    gain_key = jnp.clip(1.0 + 0.18 * jax.random.normal(key_of[4], (DH,), jnp.float32), 0.1, 1.9)
    grad_out = draw_grad_out(jax.random.fold_in(key_of[6], 71), 0)
    return dict(queries=queries, key_vectors=key_vectors, value_vectors=value_vectors, gain_query=gain_query, gain_key=gain_key, grad_out=grad_out)


eps_norm = 1e-06

def normalize(inputs, gain_vec):
    as_float = inputs.astype(jnp.float32)
    inv_rms = lax.rsqrt(lax.optimization_barrier(jnp.mean(as_float * as_float, axis=-1, keepdims=True)) + eps_norm)
    return ((as_float * inv_rms * gain_vec).astype(jnp.bfloat16), inv_rms)

def norm_backward(inputs, inv_rms, gain_vec, upstream):
    as_float = inputs.astype(jnp.float32)
    inner_mean = lax.optimization_barrier(jnp.mean(as_float * gain_vec * upstream, axis=-1, keepdims=True))
    result = inv_rms * gain_vec * upstream - as_float * inv_rms * inv_rms * inv_rms * inner_mean
    gain_part = lax.optimization_barrier(jnp.sum(as_float * inv_rms * upstream, axis=(0, 1)))
    return (result, gain_part)

def coarsen(inputs, axis_index):
    old_shape = inputs.shape
    new_shape = old_shape[:axis_index] + (old_shape[axis_index] // 2, 2) + old_shape[axis_index + 1:]
    paired = inputs.astype(jnp.float32).reshape(new_shape)
    return (0.5 * lax.optimization_barrier(jnp.sum(paired, axis=axis_index + 1))).astype(jnp.bfloat16)

def restrict(inputs, factor):
    old_shape = inputs.shape
    return lax.optimization_barrier(jnp.sum(inputs.reshape((old_shape[0] // factor, factor) + old_shape[1:]), axis=1))

def widen(running, coarse, factor):
    old_shape = running.shape
    return (running.reshape((old_shape[0] // factor, factor) + old_shape[1:]) + coarse[:, None]).reshape(old_shape)

def swap_pairs(inputs, row_count):
    old_shape = inputs.shape
    paired = inputs.reshape((old_shape[0] // (2 * row_count), 2, row_count) + old_shape[1:])
    return paired[:, ::-1].reshape(old_shape)

def blocked(inputs):
    return inputs.reshape((inputs.shape[0] // BLOCK, BLOCK) + inputs.shape[1:])

def flatten_blocks(inputs):
    return inputs.reshape((inputs.shape[0] * inputs.shape[1],) + inputs.shape[2:])

def rounded(inputs):
    return lax.optimization_barrier(inputs.astype(jnp.bfloat16)).astype(jnp.float32)

def product(formula, first_op, second_op):
    return jnp.einsum(formula, first_op.astype(jnp.float32), second_op.astype(jnp.float32), precision=lax.Precision.HIGHEST)

def level_forward(weight, operands):
    queries, key_block, value_block = operands
    inv_root = 1.0 / math.sqrt(queries.shape[-1])
    scores = product('rhd,khd->hrk', queries, key_block) * inv_root
    probabilities = jnp.exp(scores)
    numerator = weight * product('hrk,khd->rhd', rounded(probabilities), value_block)
    denominator = weight * jnp.transpose(lax.optimization_barrier(jnp.sum(probabilities, axis=-1)))
    return (numerator, denominator)

def level_backward(weight, operands):
    queries, key_block, value_block, grad_numerator, grad_denominator = operands
    inv_root = 1.0 / math.sqrt(queries.shape[-1])
    scores = product('rhd,khd->hrk', queries, key_block) * inv_root
    probabilities = jnp.exp(scores)
    scaled_numer = rounded(weight * grad_numerator)
    dvalues = product('hrk,rhd->khd', rounded(probabilities), scaled_numer)
    dprobs = product('rhd,khd->hrk', scaled_numer, value_block) + weight * jnp.transpose(grad_denominator)[:, :, None]
    dscores = rounded(probabilities * dprobs * inv_root)
    dqueries = product('hrk,khd->rhd', dscores, key_block)
    dkeys = product('hrk,rhd->khd', dscores, queries)
    return (dqueries, dkeys, dvalues)

def reference(queries, key_vectors, value_vectors, gain_query, gain_key, grad_out):
    query_heads = queries.reshape(TOKENS, HEADS, DH)
    key_heads = key_vectors.reshape(TOKENS, HEADS, DH)
    value_heads = value_vectors.reshape(TOKENS, HEADS, DH)
    query_norm, query_rms = normalize(query_heads, gain_query)
    key_norm, key_rms = normalize(key_heads, gain_key)
    query_levels = [query_norm]
    key_levels = [key_norm]
    value_levels = [value_heads]
    for level_index in range(1, LEVELS):
        query_levels.append(coarsen(query_levels[-1], 0))
        key_levels.append(coarsen(key_levels[-1], 0))
        value_levels.append(coarsen(value_levels[-1], 0))
    numer_total = jnp.zeros((TOKENS, HEADS, DH), jnp.float32)
    denom_total = jnp.zeros((TOKENS, HEADS), jnp.float32)
    diag_numer, diag_denom = lax.map(partial(level_forward, 1.0), (blocked(query_norm), blocked(key_norm), blocked(value_heads)))
    numer_total = numer_total + flatten_blocks(diag_numer)
    denom_total = denom_total + flatten_blocks(diag_denom)
    for level_index in range(LEVELS):
        factor = 1 << level_index
        level_numer, level_denom = lax.map(partial(level_forward, float(factor)), (blocked(query_levels[level_index]), blocked(swap_pairs(key_levels[level_index], BLOCK)), blocked(swap_pairs(value_levels[level_index], BLOCK))))
        numer_total = widen(numer_total, flatten_blocks(level_numer), factor)
        denom_total = widen(denom_total, flatten_blocks(level_denom), factor)
    out_float = numer_total / denom_total[..., None]
    attended = out_float.astype(jnp.bfloat16).reshape(TOKENS, HEADS * DH)
    upstream = grad_out.astype(jnp.float32).reshape(TOKENS, HEADS, DH)
    grad_numer = upstream / denom_total[..., None]
    grad_denom = -lax.optimization_barrier(jnp.sum(upstream * out_float, axis=-1)) / denom_total
    grads_query = [jnp.zeros(level_array.shape, jnp.float32) for level_array in query_levels]
    grads_key = [jnp.zeros(level_array.shape, jnp.float32) for level_array in key_levels]
    grads_value = [jnp.zeros(level_array.shape, jnp.float32) for level_array in value_levels]
    diag_dq, diag_dk, diag_dv = lax.map(partial(level_backward, 1.0), (blocked(query_norm), blocked(key_norm), blocked(value_heads), blocked(grad_numer), blocked(grad_denom)))
    grads_query[0] = grads_query[0] + flatten_blocks(diag_dq)
    grads_key[0] = grads_key[0] + flatten_blocks(diag_dk)
    grads_value[0] = grads_value[0] + flatten_blocks(diag_dv)
    for level_index in range(LEVELS):
        factor = 1 << level_index
        level_dq, level_dk, level_dv = lax.map(partial(level_backward, float(factor)), (blocked(query_levels[level_index]), blocked(swap_pairs(key_levels[level_index], BLOCK)), blocked(swap_pairs(value_levels[level_index], BLOCK)), blocked(restrict(grad_numer, factor)), blocked(restrict(grad_denom, factor))))
        grads_query[level_index] = grads_query[level_index] + flatten_blocks(level_dq)
        grads_key[level_index] = grads_key[level_index] + swap_pairs(flatten_blocks(level_dk), BLOCK)
        grads_value[level_index] = grads_value[level_index] + swap_pairs(flatten_blocks(level_dv), BLOCK)
    for level_index in reversed(range(LEVELS - 1)):
        grads_query[level_index] = grads_query[level_index] + 0.5 * jnp.repeat(grads_query[level_index + 1], 2, axis=0)
        grads_key[level_index] = grads_key[level_index] + 0.5 * jnp.repeat(grads_key[level_index + 1], 2, axis=0)
        grads_value[level_index] = grads_value[level_index] + 0.5 * jnp.repeat(grads_value[level_index + 1], 2, axis=0)
    query_result, query_gain_part = norm_backward(query_heads, query_rms, gain_query, grads_query[0])
    key_result, key_gain_part = norm_backward(key_heads, key_rms, gain_key, grads_key[0])
    gain_grads = jnp.stack([query_gain_part, key_gain_part]) / math.sqrt(TOKENS * HEADS)
    grad_query = query_result.astype(jnp.bfloat16).reshape(TOKENS, HEADS * DH)
    grad_key = key_result.astype(jnp.bfloat16).reshape(TOKENS, HEADS * DH)
    grad_value = grads_value[0].astype(jnp.bfloat16).reshape(TOKENS, HEADS * DH)
    return (attended, grad_query, grad_key, grad_value, gain_grads)
```

```python
import functools
import math

import jax
import jax.numpy as jnp
from jax import lax
from jax.experimental import pallas as pl
from jax.experimental.pallas import tpu as pltpu
from jax.sharding import PartitionSpec as P

HEADS = 16
DH = 128
QUAD = 4
EPS = 1e-06
F32 = jnp.float32
BF16 = jnp.bfloat16


def flip(index, mask):
    result = index
    bit = 0
    while mask >> bit:
        if (mask >> bit) & 1:
            own = lax.rem(lax.div(index, 1 << bit), 2)
            result = result + (1 - 2 * own) * (1 << bit)
        bit += 1
    return result


def dot_nn(a, b):
    return lax.dot_general(a, b, (((1,), (0,)), ((), ())), preferred_element_type=F32)


def dot_nt(a, b):
    return lax.dot_general(a, b, (((1,), (1,)), ((), ())), preferred_element_type=F32)


def dot_tn(a, b):
    return lax.dot_general(a, b, (((0,), (0,)), ((), ())), preferred_element_type=F32)


def unrolled(count, step):
    for i in range(count):
        step(i, 0)


def tiled(lanes, width):
    return jnp.concatenate([lanes] * (width // lanes.shape[1]), axis=1)


def kernel(
    seq_count, rows, own_heads,
    q_hbm, k_hbm, v_hbm, g_hbm, gain_q, gain_k,
    att_hbm, dq_hbm, dk_hbm, dv_hbm, gain_out,
    rin, oout, qp, kvp, rkv, gsend, grecv, wide, num, den, gnp, gdp, gqp, gkp, gvp,
    pair_p, one_p, up_p, gains, gacc, gsum, ga, gb, gc, rms,
    in_s, in_r, out_s, out_r, kv_s, kv_r, gr_s, gr_r, ga_s, ga_r, gb_s, gb_r, gc_s, gc_r, gain_s, ready,
):
    depth = seq_count.bit_length() - 1
    groups = seq_count // QUAD
    total = QUAD * rows
    inv_root = 1.0 / math.sqrt(DH)
    exp_scale = inv_root * math.log2(math.e)
    level_rows = [total >> j for j in range(depth)]
    offs = [2 * total - 2 * (total >> j) for j in range(depth)]
    me = lax.axis_index("seq")
    core = lax.axis_index("head")
    member = lax.rem(me, QUAD)
    group = lax.div(me, QUAD)
    inputs = (q_hbm, k_hbm, v_hbm, g_hbm)
    outputs = (att_hbm, dq_hbm, dk_hbm, dv_hbm)

    def col(index, h):
        return pl.ds(pl.multiple_of((index * own_heads + h) * DH, DH), DH)

    def rowset(index):
        return pl.ds(pl.multiple_of(index * rows, rows), rows)

    def in_copy(a, h, x):
        if x == 0:
            return pltpu.make_async_copy(
                inputs[a].at[:, col(member, h)], rin.at[a, h, rowset(member)], in_r.at[a, h, 0]
            )
        return pltpu.make_async_remote_copy(
            inputs[a].at[:, col(flip(member, x), h)],
            rin.at[a, h, rowset(member)],
            in_s.at[a, h, x],
            in_r.at[a, h, x],
            device_id={"seq": flip(me, x)},
            device_id_type=pl.DeviceIdType.MESH,
        )

    def out_copy(a, h, x):
        if x == 0:
            return pltpu.make_async_copy(
                oout.at[a, h, rowset(member)], outputs[a].at[:, col(member, h)], out_r.at[a, h, 0]
            )
        return pltpu.make_async_remote_copy(
            oout.at[a, h, rowset(flip(member, x))],
            outputs[a].at[:, col(member, h)],
            out_s.at[a, h, x],
            out_r.at[a, h, x],
            device_id={"seq": flip(me, x)},
            device_id_type=pl.DeviceIdType.MESH,
        )

    def peer_level(d):
        j = 1 + d.bit_length()
        return j, d - (1 << (j - 2))

    def kv_copy(h, d):
        j, t = peer_level(d)
        n = level_rows[j]
        return pltpu.make_async_remote_copy(
            kvp.at[h, :, pl.ds(offs[j], n)],
            rkv.at[h, j - 2, :, pl.ds(t * n, n)],
            kv_s.at[h, d],
            kv_r.at[h, d],
            device_id={"seq": flip(me, QUAD * d)},
            device_id_type=pl.DeviceIdType.MESH,
        )

    def grad_copy(h, d):
        j, t = peer_level(d)
        n = level_rows[j]
        return pltpu.make_async_remote_copy(
            gsend.at[h, j - 2, :, pl.ds(t * n, n)],
            grecv.at[h, j - 2, :, pl.ds(t * n, n)],
            gr_s.at[h, d],
            gr_r.at[h, d],
            device_id={"seq": flip(me, QUAD * d)},
            device_id_type=pl.DeviceIdType.MESH,
        )

    barrier = pltpu.get_barrier_semaphore()
    for x in range(1, QUAD):
        pl.semaphore_signal(
            barrier, inc=1, device_id={"seq": flip(me, x)}, device_id_type=pl.DeviceIdType.MESH
        )
    pl.semaphore_signal(
        barrier, inc=1, device_id={"head": 1 - core}, device_id_type=pl.DeviceIdType.MESH
    )
    pl.semaphore_wait(barrier, QUAD + group)

    def greet(semaphore):
        def step(other, _):
            pl.semaphore_signal(
                semaphore,
                inc=1,
                device_id={"seq": other * QUAD + member},
                device_id_type=pl.DeviceIdType.MESH,
            )
            return 0

        return step

    lax.fori_loop(group + 1, groups, greet(barrier), 0)
    lax.fori_loop(0, group, greet(ready), 0)

    for h in range(own_heads):
        for a in (1, 2, 0, 3):
            for x in (3, 1, 2, 0):
                in_copy(a, h, x).start()

    gain_loads = [
        pltpu.make_async_copy(src, gains.at[i], gain_s.at[i]) for i, src in enumerate((gain_q, gain_k))
    ]
    for load in gain_loads:
        load.start()
    for load in gain_loads:
        load.wait()
    gacc[...] = jnp.zeros_like(gacc)

    def wait_in(a, h):
        for x in range(1, QUAD):
            in_copy(a, h, x).wait_recv()
        in_copy(a, h, 0).wait()

    def norm_rows(raw):
        as_float = raw.astype(F32)
        inv = lax.rsqrt(jnp.mean(as_float * as_float, axis=-1, keepdims=True) + EPS)
        return as_float, inv

    chunks = total // rows

    def pyramid(read, write):
        def base(c, _):
            r = pl.ds(c * rows, rows)
            value = read(r)
            write(r, value)
            wide[r] = value.astype(F32)

        unrolled(chunks, base)
        for j in range(1, depth):
            n = level_rows[j]
            step = min(n, 256)
            for s in range(0, n, step):
                mean = 0.5 * (
                    wide[pl.ds(2 * s, step, stride=2)] + wide[pl.ds(2 * s + 1, step, stride=2)]
                )
                value = mean.astype(BF16)
                write(pl.ds(offs[j] + s, step), value)
                wide[pl.ds(s, step)] = value.astype(F32)

    def spread(ref, j, factor):
        n = level_rows[j]
        step = min(n, 256)
        for s in range(0, n, step):
            value = factor * ref[pl.ds(offs[j] + s, step)]
            for parity in range(2):
                dst = pl.ds(offs[j - 1] + 2 * s + parity, step, stride=2)
                ref[dst] = ref[dst] + value

    def gather_pairs(ref, j):
        n = level_rows[j]
        step = min(n, 256)
        for s in range(0, n, step):
            first = ref[pl.ds(offs[j - 1] + 2 * s, step, stride=2)]
            second = ref[pl.ds(offs[j - 1] + 2 * s + 1, step, stride=2)]
            ref[pl.ds(offs[j] + s, step)] = first + second

    def probs(q, k):
        return jnp.exp2(dot_nt(q, k) * exp_scale)

    def forward(weight, r, q, k, v):
        p = probs(q, k)
        pb = p.astype(BF16)
        both = dot_nn(pb, jnp.concatenate([v, jnp.ones_like(v)], axis=1))
        num[r] = weight * both[:, :DH]
        den[r] = weight * both[:, DH:]
        return pb

    def backward(weight, h, r, pb, q, k, v):
        sn = (weight * gnp[h, r]).astype(BF16)
        dv = dot_tn(pb, sn)
        dp = dot_nt(sn, v) + tiled(weight * gdp[h, r], k.shape[0])
        ds = (pb.astype(F32) * dp).astype(BF16)
        dq = inv_root * dot_nn(ds, k)
        dk = inv_root * dot_tn(ds, q)
        return dq, dk, dv

    def gain_copies(src, landing, sends, recvs, peers):
        return [
            pltpu.make_async_remote_copy(
                src,
                landing.at[i],
                sends.at[i],
                recvs.at[i],
                device_id=peer,
                device_id_type=pl.DeviceIdType.MESH,
            )
            for i, peer in enumerate(peers)
        ]

    quad_gains = gain_copies(gacc, ga, ga_s, ga_r, [{"seq": flip(me, x)} for x in range(1, QUAD)])
    group_gains = gain_copies(
        gsum.at[0], gb, gb_s, gb_r, [{"seq": flip(me, QUAD * d)} for d in range(1, groups)]
    )
    core_gains = gain_copies(gsum.at[1], gc, gc_s, gc_r, [{"head": 1 - core}])

    gq = gains[0]
    gk = gains[1]

    def keys_and_values(h, _):
        def read_k(r):
            as_float, inv = norm_rows(rin[1, h, r])
            rms[1, h, r] = jnp.broadcast_to(inv, as_float.shape)
            return (as_float * inv * gk).astype(BF16)

        def write_k(r, value):
            kvp[h, 0, r] = value

        def write_v(r, value):
            kvp[h, 1, r] = value

        wait_in(1, h)
        pyramid(read_k, write_k)
        wait_in(2, h)
        pyramid(lambda r: rin[2, h, r], write_v)
        if h == 0:

            @pl.when(group < groups - 1)
            def _():
                pl.semaphore_wait(ready, groups - 1 - group)

        for d in range(1, groups):
            kv_copy(h, d).start()
        return 0

    def forward_pass(h, _):
        def read_q(r):
            as_float, inv = norm_rows(rin[0, h, r])
            rms[0, h, r] = jnp.broadcast_to(inv, as_float.shape)
            return (as_float * inv * gq).astype(BF16)

        def write_q(r, value):
            qp[h, r] = value

        wait_in(0, h)
        pyramid(read_q, write_q)

        def pair_forward(b, _):
            r = pl.ds(b * 2 * rows, 2 * rows)
            pair_p[h, r] = forward(1.0, r, qp[h, r], kvp[h, 0, r], kvp[h, 1, r])

        unrolled(chunks // 2, pair_forward)

        def one_forward(b, _):
            r = pl.ds(offs[1] + b * rows, rows)
            keys = pl.ds(offs[1] + (1 - b) * rows, rows)
            one_p[h, b] = forward(2.0, r, qp[h, r], kvp[h, 0, keys], kvp[h, 1, keys])

        unrolled(2, one_forward)
        for d in range(1, groups):
            kv_copy(h, d).wait_recv()
        for j in range(2, depth):
            r = pl.ds(offs[j], level_rows[j])
            up_p[j - 2, pl.ds(0, level_rows[j])] = forward(
                float(1 << j), r, qp[h, r], rkv[h, j - 2, 0], rkv[h, j - 2, 1]
            )
        for j in reversed(range(1, depth)):
            spread(num, j, 1.0)
            spread(den, j, 1.0)

        wait_in(3, h)

        def middle(c, _):
            r = pl.ds(pl.multiple_of(c * rows, rows), rows)
            inv = 1.0 / den[r]
            out_float = num[r] * inv
            oout[0, h, r] = out_float.astype(BF16)
            up = rin[3, h, r].astype(F32)
            gnp[h, r] = up * inv
            gdp[h, r] = -jnp.sum(up * out_float, axis=-1, keepdims=True) * inv
            return 0

        lax.fori_loop(0, chunks, middle, 0)
        for x in range(QUAD):
            out_copy(0, h, x).start()
        for j in range(1, depth):
            gather_pairs(gnp.at[h], j)
            gather_pairs(gdp.at[h], j)

        for j in range(2, depth):
            r = pl.ds(offs[j], level_rows[j])
            dq, dk, dv = backward(
                float(1 << j),
                h,
                r,
                up_p[j - 2, pl.ds(0, level_rows[j])],
                qp[h, r],
                rkv[h, j - 2, 0],
                rkv[h, j - 2, 1],
            )
            gqp[h, r] = dq
            gsend[h, j - 2, 0] = dk.astype(BF16)
            gsend[h, j - 2, 1] = dv.astype(BF16)
        for d in range(1, groups):
            grad_copy(h, d).start()
        return 0

    def norm_back(a, h, src, gain, row):
        some = min(rows, 128)

        def step(c, acc):
            r = pl.ds(pl.multiple_of(c * some, some), some)
            inv = rms[a, h, r]
            normed = rin[a, h, r].astype(F32) * inv
            scaled = gain * src[r]
            both = normed * scaled
            inner = jnp.mean(both, axis=-1, keepdims=True)
            oout[1 + a, h, r] = (inv * (scaled - normed * inner)).astype(BF16)
            return acc + jnp.sum(both.reshape(some // 8, 8, DH), axis=0)

        part = lax.fori_loop(0, total // some, step, jnp.zeros((8, DH), F32), unroll=2)
        part = jnp.sum(part, axis=0, keepdims=True) / gain
        gacc[row : row + 1] = gacc[row : row + 1] + part
        if h == own_heads - 1 and row == 1:
            for copy in quad_gains:
                copy.start()
            for held in (1,):
                for x in range(QUAD):
                    out_copy(held, h, x).start()
        if h < own_heads - 1 or row == 1:
            for x in range(QUAD):
                out_copy(1 + a, h, x).start()

    def backward_queries(h):
        def one_backward(b, _):
            r = pl.ds(offs[1] + b * rows, rows)
            keys = pl.ds(offs[1] + (1 - b) * rows, rows)
            dq, dk, dv = backward(
                2.0, h, r, one_p[h, b], qp[h, r], kvp[h, 0, keys], kvp[h, 1, keys]
            )
            gqp[h, r] = dq
            gkp[keys] = dk
            gvp[keys] = dv

        unrolled(2, one_backward)

        def pair_backward(b, _):
            r = pl.ds(b * 2 * rows, 2 * rows)
            dq, dk, dv = backward(
                1.0, h, r, pair_p[h, r], qp[h, r], kvp[h, 0, r], kvp[h, 1, r]
            )
            gqp[h, r] = dq
            gkp[r] = dk
            gvp[r] = dv

        unrolled(chunks // 2, pair_backward)
        for j in reversed(range(1, depth)):
            spread(gqp.at[h], j, 0.5)

        norm_back(0, h, gqp.at[h], gq, 0)

    def backward_keys(h):
        for d in range(1, groups):
            grad_copy(h, d).wait_recv()
        for ref, which in ((gkp, 0), (gvp, 1)):
            for j in range(2, depth):
                n = level_rows[j]
                summed = grecv[h, j - 2, which, pl.ds(0, n)].astype(F32)
                for t in range(1, 1 << (j - 2)):
                    summed = summed + grecv[h, j - 2, which, pl.ds(t * n, n)].astype(F32)
                ref[pl.ds(offs[j], n)] = summed
            for j in reversed(range(1, depth)):
                spread(ref, j, 0.5)
            if which == 0:
                norm_back(1, h, gkp, gk, 1)

        def value_out(c, _):
            r = pl.ds(pl.multiple_of(c * rows, rows), rows)
            oout[3, h, r] = gvp[r].astype(BF16)
            return 0

        lax.fori_loop(0, chunks, value_out, 0)
        for x in range(QUAD):
            out_copy(3, h, x).start()

    for h in range(own_heads):
        keys_and_values(h, 0)
        if h:
            backward_queries(h - 1)
        forward_pass(h, 0)
        if h:
            backward_keys(h - 1)
    backward_queries(own_heads - 1)
    backward_keys(own_heads - 1)

    total_gain = gacc[...]
    for round, (copies, landing) in enumerate(((quad_gains, ga), (group_gains, gb), (core_gains, gc))):
        if round:
            gsum[round - 1] = total_gain
            for copy in copies:
                copy.start()
        for copy in copies:
            copy.wait()
        for i in range(len(copies)):
            total_gain = total_gain + landing[i]
    gain_out[...] = total_gain[0:2] * (1.0 / math.sqrt(rows * seq_count * HEADS))

    def finish(h, _):
        for a in range(4):
            for x in range(1, QUAD):
                in_copy(a, h, x).wait_send()
                out_copy(a, h, x).wait_send()
                out_copy(a, h, x).wait_recv()
            out_copy(a, h, 0).wait()
        for d in range(1, groups):
            kv_copy(h, d).wait_send()
            grad_copy(h, d).wait_send()
        return 0

    lax.fori_loop(0, own_heads, finish, 0)


def store_kernel(a0, a1, a2, a3, gains, o0, o1, o2, o3, gains_out, sems):
    copies = [
        pltpu.make_async_copy(src, dst, sems.at[i])
        for i, (src, dst) in enumerate(((a0, o0), (a1, o1), (a2, o2), (a3, o3)))
    ]
    for copy in copies:
        copy.start()
    gains_out[...] = gains[...]
    for copy in copies:
        copy.wait()


def per_device(queries, key_vectors, value_vectors, gain_query, gain_key, grad_out):
    rows, width = queries.shape
    seq_count = lax.axis_size("seq")
    own_heads = width // DH // QUAD
    depth = seq_count.bit_length() - 1
    groups = seq_count // QUAD
    total = QUAD * rows
    ups = max(depth - 2, 1)
    dma = pltpu.SemaphoreType.DMA
    any_spec = pl.BlockSpec(memory_space=pl.ANY)
    hbm_spec = pl.BlockSpec(memory_space=pltpu.HBM)
    vmem_spec = pl.BlockSpec(memory_space=pltpu.VMEM)
    like = jax.ShapeDtypeStruct((rows, width), BF16)
    out = pl.pallas_call(
        functools.partial(kernel, seq_count, rows, own_heads),
        out_shape=(like, like, like, like, jax.ShapeDtypeStruct((2, DH), F32)),
        in_specs=[hbm_spec] * 6,
        out_specs=(any_spec,) * 4 + (vmem_spec,),
        scratch_shapes=[
            pltpu.VMEM((4, own_heads, total, DH), BF16),
            pltpu.VMEM((4, own_heads, total, DH), BF16),
            pltpu.VMEM((own_heads, 2 * total, DH), BF16),
            pltpu.VMEM((own_heads, 2, 2 * total, DH), BF16),
            pltpu.VMEM((own_heads, ups, 2, rows, DH), BF16),
            pltpu.VMEM((own_heads, ups, 2, rows, DH), BF16),
            pltpu.VMEM((own_heads, ups, 2, rows, DH), BF16),
            pltpu.VMEM((total, DH), F32),
            pltpu.VMEM((2 * total, DH), F32),
            pltpu.VMEM((2 * total, DH), F32),
            pltpu.VMEM((own_heads, 2 * total, DH), F32),
            pltpu.VMEM((own_heads, 2 * total, DH), F32),
            pltpu.VMEM((own_heads, 2 * total, DH), F32),
            pltpu.VMEM((2 * total, DH), F32),
            pltpu.VMEM((2 * total, DH), F32),
            pltpu.VMEM((own_heads, total, 2 * rows), BF16),
            pltpu.VMEM((own_heads, 2, rows, rows), BF16),
            pltpu.VMEM((ups, rows, rows), BF16),
            pltpu.VMEM((2, 1, DH), F32),
            pltpu.VMEM((8, DH), F32),
            pltpu.VMEM((2, 8, DH), F32),
            pltpu.VMEM((QUAD, 8, DH), F32),
            pltpu.VMEM((groups, 8, DH), F32),
            pltpu.VMEM((1, 8, DH), F32),
            pltpu.VMEM((2, own_heads, total, DH), F32),
        ]
        + [dma((4, own_heads, QUAD))] * 4
        + [dma((own_heads, groups))] * 4
        + [dma((QUAD,))] * 2
        + [dma((groups,))] * 2
        + [dma((1,))] * 2
        + [dma((2,)), pltpu.SemaphoreType.REGULAR],
        compiler_params=pltpu.CompilerParams(
            collective_id=0, has_side_effects=True, vmem_limit_bytes=48 << 20
        ),
    )(
        *(
            pltpu.with_memory_space_constraint(x, pltpu.HBM)
            for x in (
                queries, key_vectors, value_vectors, grad_out,
                gain_query.reshape(1, DH), gain_key.reshape(1, DH),
            )
        )
    )
    return pl.pallas_call(
        store_kernel,
        out_shape=(like, like, like, like, jax.ShapeDtypeStruct((2, DH), F32)),
        in_specs=[any_spec] * 4 + [vmem_spec],
        out_specs=(hbm_spec,) * 4 + (vmem_spec,),
        scratch_shapes=[dma((4,))],
        compiler_params=pltpu.CompilerParams(vmem_limit_bytes=4 << 20),
    )(*out)


def solution(mesh):
    in_specs = (P("seq", "head"), P("seq", "head"), P("seq", "head"), P(), P(), P("seq", "head"))
    out_specs = (P("seq", "head"), P("seq", "head"), P("seq", "head"), P("seq", "head"), P())
    return jax.shard_map(
        per_device, mesh=mesh, in_specs=in_specs, out_specs=out_specs, check_vma=False
    )
```

```python
import functools
import math

import jax
import jax.numpy as jnp
from jax import lax
from jax.experimental import pallas as pl
from jax.experimental.pallas import tpu as pltpu
from jax.sharding import PartitionSpec as P

HEADS = 16
DH = 128
QUAD = 4
EPS = 1e-06
F32 = jnp.float32
BF16 = jnp.bfloat16


def flip(index, mask):
    result = index
    bit = 0
    while mask >> bit:
        if (mask >> bit) & 1:
            own = lax.rem(lax.div(index, 1 << bit), 2)
            result = result + (1 - 2 * own) * (1 << bit)
        bit += 1
    return result


def dot_nn(a, b):
    return lax.dot_general(a, b, (((1,), (0,)), ((), ())), preferred_element_type=F32)


def dot_nt(a, b):
    return lax.dot_general(a, b, (((1,), (1,)), ((), ())), preferred_element_type=F32)


def dot_tn(a, b):
    return lax.dot_general(a, b, (((0,), (0,)), ((), ())), preferred_element_type=F32)


def unrolled(count, step):
    for i in range(count):
        step(i, 0)


def tiled(lanes, width):
    return jnp.concatenate([lanes] * (width // lanes.shape[1]), axis=1)


def kernel(
    seq_count, rows, own_heads,
    q_hbm, k_hbm, v_hbm, g_hbm, gain_q, gain_k,
    att_hbm, dq_hbm, dk_hbm, dv_hbm, gain_out,
    rin, oout, qp, kvp, rkv, gsend, grecv, wide, num, den, gnp, gdp, gqp, gkp, gvp,
    pair_p, one_p, up_p, gains, gacc, gsum, ga, gb, gc, rms,
    in_s, in_r, out_s, out_r, kv_s, kv_r, gr_s, gr_r, ga_s, ga_r, gb_s, gb_r, gc_s, gc_r, gain_s, ready,
):
    depth = seq_count.bit_length() - 1
    groups = seq_count // QUAD
    total = QUAD * rows
    inv_root = 1.0 / math.sqrt(DH)
    exp_scale = inv_root * math.log2(math.e)
    level_rows = [total >> j for j in range(depth)]
    offs = [2 * total - 2 * (total >> j) for j in range(depth)]
    me = lax.axis_index("seq")
    core = lax.axis_index("head")
    member = lax.rem(me, QUAD)
    group = lax.div(me, QUAD)
    inputs = (q_hbm, k_hbm, v_hbm, g_hbm)
    outputs = (att_hbm, dq_hbm, dk_hbm, dv_hbm)

    def col(index, h):
        return pl.ds(pl.multiple_of((index * own_heads + h) * DH, DH), DH)

    def rowset(index):
        return pl.ds(pl.multiple_of(index * rows, rows), rows)

    def in_copy(a, h, x):
        if x == 0:
            return pltpu.make_async_copy(
                inputs[a].at[:, col(member, h)], rin.at[a, h, rowset(member)], in_r.at[a, h, 0]
            )
        return pltpu.make_async_remote_copy(
            inputs[a].at[:, col(flip(member, x), h)],
            rin.at[a, h, rowset(member)],
            in_s.at[a, h, x],
            in_r.at[a, h, x],
            device_id={"seq": flip(me, x)},
            device_id_type=pl.DeviceIdType.MESH,
        )

    def out_copy(a, h, x):
        if x == 0:
            return pltpu.make_async_copy(
                oout.at[a, h, rowset(member)], outputs[a].at[:, col(member, h)], out_r.at[a, h, 0]
            )
        return pltpu.make_async_remote_copy(
            oout.at[a, h, rowset(flip(member, x))],
            outputs[a].at[:, col(member, h)],
            out_s.at[a, h, x],
            out_r.at[a, h, x],
            device_id={"seq": flip(me, x)},
            device_id_type=pl.DeviceIdType.MESH,
        )

    def peer_level(d):
        j = 1 + d.bit_length()
        return j, d - (1 << (j - 2))

    def kv_copy(h, d):
        j, t = peer_level(d)
        n = level_rows[j]
        return pltpu.make_async_remote_copy(
            kvp.at[h, :, pl.ds(offs[j], n)],
            rkv.at[h, j - 2, :, pl.ds(t * n, n)],
            kv_s.at[h, d],
            kv_r.at[h, d],
            device_id={"seq": flip(me, QUAD * d)},
            device_id_type=pl.DeviceIdType.MESH,
        )

    def grad_copy(h, d):
        j, t = peer_level(d)
        n = level_rows[j]
        return pltpu.make_async_remote_copy(
            gsend.at[h, j - 2, :, pl.ds(t * n, n)],
            grecv.at[h, j - 2, :, pl.ds(t * n, n)],
            gr_s.at[h, d],
            gr_r.at[h, d],
            device_id={"seq": flip(me, QUAD * d)},
            device_id_type=pl.DeviceIdType.MESH,
        )

    barrier = pltpu.get_barrier_semaphore()
    for x in range(1, QUAD):
        pl.semaphore_signal(
            barrier, inc=1, device_id={"seq": flip(me, x)}, device_id_type=pl.DeviceIdType.MESH
        )
    pl.semaphore_signal(
        barrier, inc=1, device_id={"head": 1 - core}, device_id_type=pl.DeviceIdType.MESH
    )
    pl.semaphore_wait(barrier, QUAD + group)

    def greet(semaphore):
        def step(other, _):
            pl.semaphore_signal(
                semaphore,
                inc=1,
                device_id={"seq": other * QUAD + member},
                device_id_type=pl.DeviceIdType.MESH,
            )
            return 0

        return step

    lax.fori_loop(group + 1, groups, greet(barrier), 0)
    lax.fori_loop(0, group, greet(ready), 0)

    for pair in ((1, 2), (0, 3)):
        for h in range(own_heads):
            for a in pair:
                for x in (3, 1, 2, 0):
                    in_copy(a, h, x).start()

    gain_loads = [
        pltpu.make_async_copy(src, gains.at[i], gain_s.at[i]) for i, src in enumerate((gain_q, gain_k))
    ]
    for load in gain_loads:
        load.start()
    for load in gain_loads:
        load.wait()
    gacc[...] = jnp.zeros_like(gacc)

    def wait_in(a, h):
        for x in range(1, QUAD):
            in_copy(a, h, x).wait_recv()
        in_copy(a, h, 0).wait()

    def norm_rows(raw):
        as_float = raw.astype(F32)
        inv = lax.rsqrt(jnp.mean(as_float * as_float, axis=-1, keepdims=True) + EPS)
        return as_float, inv

    chunks = total // rows

    def pyramid(read, write):
        def base(c, _):
            r = pl.ds(c * rows, rows)
            value = read(r)
            write(r, value)
            wide[r] = value.astype(F32)

        unrolled(chunks, base)
        for j in range(1, depth):
            n = level_rows[j]
            step = min(n, 256)
            for s in range(0, n, step):
                mean = 0.5 * (
                    wide[pl.ds(2 * s, step, stride=2)] + wide[pl.ds(2 * s + 1, step, stride=2)]
                )
                value = mean.astype(BF16)
                write(pl.ds(offs[j] + s, step), value)
                wide[pl.ds(s, step)] = value.astype(F32)

    def spread(ref, j, factor):
        n = level_rows[j]
        step = min(n, 256)
        for s in range(0, n, step):
            value = factor * ref[pl.ds(offs[j] + s, step)]
            for parity in range(2):
                dst = pl.ds(offs[j - 1] + 2 * s + parity, step, stride=2)
                ref[dst] = ref[dst] + value

    def gather_pairs(ref, j):
        n = level_rows[j]
        step = min(n, 256)
        for s in range(0, n, step):
            first = ref[pl.ds(offs[j - 1] + 2 * s, step, stride=2)]
            second = ref[pl.ds(offs[j - 1] + 2 * s + 1, step, stride=2)]
            ref[pl.ds(offs[j] + s, step)] = first + second

    def probs(q, k):
        return jnp.exp2(dot_nt(q, k) * exp_scale)

    def forward(weight, r, q, k, v):
        p = probs(q, k)
        pb = p.astype(BF16)
        both = dot_nn(pb, jnp.concatenate([v, jnp.ones_like(v)], axis=1))
        num[r] = weight * both[:, :DH]
        den[r] = weight * both[:, DH:]
        return pb

    def backward(weight, h, r, pb, q, k, v):
        sn = (weight * gnp[h, r]).astype(BF16)
        dv = dot_tn(pb, sn)
        dp = dot_nt(sn, v) + tiled(weight * gdp[h, r], k.shape[0])
        ds = (pb.astype(F32) * dp).astype(BF16)
        dq = inv_root * dot_nn(ds, k)
        dk = inv_root * dot_tn(ds, q)
        return dq, dk, dv

    def gain_copies(src, landing, sends, recvs, peers):
        return [
            pltpu.make_async_remote_copy(
                src,
                landing.at[i],
                sends.at[i],
                recvs.at[i],
                device_id=peer,
                device_id_type=pl.DeviceIdType.MESH,
            )
            for i, peer in enumerate(peers)
        ]

    quad_gains = gain_copies(gacc, ga, ga_s, ga_r, [{"seq": flip(me, x)} for x in range(1, QUAD)])
    group_gains = gain_copies(
        gsum.at[0], gb, gb_s, gb_r, [{"seq": flip(me, QUAD * d)} for d in range(1, groups)]
    )
    core_gains = gain_copies(gsum.at[1], gc, gc_s, gc_r, [{"head": 1 - core}])

    gq = gains[0]
    gk = gains[1]

    def keys_and_values(h, _):
        def read_k(r):
            as_float, inv = norm_rows(rin[1, h, r])
            rms[1, h, r] = jnp.broadcast_to(inv, as_float.shape)
            return (as_float * inv * gk).astype(BF16)

        def write_k(r, value):
            kvp[h, 0, r] = value

        def write_v(r, value):
            kvp[h, 1, r] = value

        wait_in(1, h)
        pyramid(read_k, write_k)
        wait_in(2, h)
        pyramid(lambda r: rin[2, h, r], write_v)
        if h == 0:

            @pl.when(group < groups - 1)
            def _():
                pl.semaphore_wait(ready, groups - 1 - group)

        for d in reversed(range(1, groups)):
            kv_copy(h, d).start()
        return 0

    def forward_pass(h, _):
        def read_q(r):
            as_float, inv = norm_rows(rin[0, h, r])
            rms[0, h, r] = jnp.broadcast_to(inv, as_float.shape)
            return (as_float * inv * gq).astype(BF16)

        def write_q(r, value):
            qp[h, r] = value

        wait_in(0, h)
        pyramid(read_q, write_q)

        def pair_forward(b, _):
            r = pl.ds(b * 2 * rows, 2 * rows)
            pair_p[h, r] = forward(1.0, r, qp[h, r], kvp[h, 0, r], kvp[h, 1, r])

        unrolled(chunks // 2, pair_forward)

        def one_forward(b, _):
            r = pl.ds(offs[1] + b * rows, rows)
            keys = pl.ds(offs[1] + (1 - b) * rows, rows)
            one_p[h, b] = forward(2.0, r, qp[h, r], kvp[h, 0, keys], kvp[h, 1, keys])

        unrolled(2, one_forward)
        for d in range(1, groups):
            kv_copy(h, d).wait_recv()
        for j in range(2, depth):
            r = pl.ds(offs[j], level_rows[j])
            up_p[j - 2, pl.ds(0, level_rows[j])] = forward(
                float(1 << j), r, qp[h, r], rkv[h, j - 2, 0], rkv[h, j - 2, 1]
            )
        for j in reversed(range(1, depth)):
            spread(num, j, 1.0)
            spread(den, j, 1.0)

        wait_in(3, h)

        def middle(c, _):
            r = pl.ds(pl.multiple_of(c * rows, rows), rows)
            inv = 1.0 / den[r]
            out_float = num[r] * inv
            oout[0, h, r] = out_float.astype(BF16)
            up = rin[3, h, r].astype(F32)
            gnp[h, r] = up * inv
            gdp[h, r] = -jnp.sum(up * out_float, axis=-1, keepdims=True) * inv
            return 0

        lax.fori_loop(0, chunks, middle, 0)
        if h < own_heads - 1:
            for x in range(QUAD):
                out_copy(0, h, x).start()
        for j in range(1, depth):
            gather_pairs(gnp.at[h], j)
            gather_pairs(gdp.at[h], j)

        for j in range(2, depth):
            r = pl.ds(offs[j], level_rows[j])
            dq, dk, dv = backward(
                float(1 << j),
                h,
                r,
                up_p[j - 2, pl.ds(0, level_rows[j])],
                qp[h, r],
                rkv[h, j - 2, 0],
                rkv[h, j - 2, 1],
            )
            gqp[h, r] = dq
            gsend[h, j - 2, 0] = dk.astype(BF16)
            gsend[h, j - 2, 1] = dv.astype(BF16)
        for d in reversed(range(1, groups)):
            grad_copy(h, d).start()
        return 0

    def norm_back(a, h, src, gain, row):
        some = min(rows, 128)

        def step(c, acc):
            r = pl.ds(pl.multiple_of(c * some, some), some)
            inv = rms[a, h, r]
            normed = rin[a, h, r].astype(F32) * inv
            scaled = gain * src[r]
            both = normed * scaled
            inner = jnp.mean(both, axis=-1, keepdims=True)
            oout[1 + a, h, r] = (inv * (scaled - normed * inner)).astype(BF16)
            return acc + jnp.sum(both.reshape(some // 8, 8, DH), axis=0)

        part = lax.fori_loop(0, total // some, step, jnp.zeros((8, DH), F32), unroll=2)
        part = jnp.sum(part, axis=0, keepdims=True) / gain
        gacc[row : row + 1] = gacc[row : row + 1] + part
        if h == own_heads - 1 and row == 1:
            for copy in quad_gains:
                copy.start()
            for held in (0, 1):
                for x in range(QUAD):
                    out_copy(held, h, x).start()
        if h < own_heads - 1 or row == 1:
            for x in range(QUAD):
                out_copy(1 + a, h, x).start()

    def backward_queries(h):
        def one_backward(b, _):
            r = pl.ds(offs[1] + b * rows, rows)
            keys = pl.ds(offs[1] + (1 - b) * rows, rows)
            dq, dk, dv = backward(
                2.0, h, r, one_p[h, b], qp[h, r], kvp[h, 0, keys], kvp[h, 1, keys]
            )
            gqp[h, r] = dq
            gkp[keys] = dk
            gvp[keys] = dv

        unrolled(2, one_backward)

        def pair_backward(b, _):
            r = pl.ds(b * 2 * rows, 2 * rows)
            dq, dk, dv = backward(
                1.0, h, r, pair_p[h, r], qp[h, r], kvp[h, 0, r], kvp[h, 1, r]
            )
            gqp[h, r] = dq
            gkp[r] = dk
            gvp[r] = dv

        unrolled(chunks // 2, pair_backward)
        for j in reversed(range(1, depth)):
            spread(gqp.at[h], j, 0.5)

        norm_back(0, h, gqp.at[h], gq, 0)

    def backward_keys(h):
        for d in range(1, groups):
            grad_copy(h, d).wait_recv()
        for ref, which in ((gkp, 0), (gvp, 1)):
            for j in range(2, depth):
                n = level_rows[j]
                summed = grecv[h, j - 2, which, pl.ds(0, n)].astype(F32)
                for t in range(1, 1 << (j - 2)):
                    summed = summed + grecv[h, j - 2, which, pl.ds(t * n, n)].astype(F32)
                ref[pl.ds(offs[j], n)] = summed
            for j in reversed(range(1, depth)):
                spread(ref, j, 0.5)
            if which == 0:
                norm_back(1, h, gkp, gk, 1)

        def value_out(c, _):
            r = pl.ds(pl.multiple_of(c * rows, rows), rows)
            oout[3, h, r] = gvp[r].astype(BF16)
            return 0

        lax.fori_loop(0, chunks, value_out, 0)
        for x in range(QUAD):
            out_copy(3, h, x).start()

    for h in range(own_heads):
        keys_and_values(h, 0)
    for h in range(own_heads):
        if h:
            backward_queries(h - 1)
        forward_pass(h, 0)
        if h:
            backward_keys(h - 1)
    backward_queries(own_heads - 1)
    backward_keys(own_heads - 1)

    total_gain = gacc[...]
    for round, (copies, landing) in enumerate(((quad_gains, ga), (group_gains, gb), (core_gains, gc))):
        if round:
            gsum[round - 1] = total_gain
            for copy in copies:
                copy.start()
        for copy in copies:
            copy.wait()
        for i in range(len(copies)):
            total_gain = total_gain + landing[i]
    gain_out[...] = total_gain[0:2] * (1.0 / math.sqrt(rows * seq_count * HEADS))

    def finish(h, _):
        for a in range(4):
            for x in range(1, QUAD):
                in_copy(a, h, x).wait_send()
                out_copy(a, h, x).wait_send()
                out_copy(a, h, x).wait_recv()
            out_copy(a, h, 0).wait()
        for d in range(1, groups):
            kv_copy(h, d).wait_send()
            grad_copy(h, d).wait_send()
        return 0

    lax.fori_loop(0, own_heads, finish, 0)


def store_kernel(a0, a1, a2, a3, gains, o0, o1, o2, o3, gains_out, sems):
    copies = [
        pltpu.make_async_copy(src, dst, sems.at[i])
        for i, (src, dst) in enumerate(((a0, o0), (a1, o1), (a2, o2), (a3, o3)))
    ]
    for copy in copies:
        copy.start()
    gains_out[...] = gains[...]
    for copy in copies:
        copy.wait()


def per_device(queries, key_vectors, value_vectors, gain_query, gain_key, grad_out):
    rows, width = queries.shape
    seq_count = lax.axis_size("seq")
    own_heads = width // DH // QUAD
    depth = seq_count.bit_length() - 1
    groups = seq_count // QUAD
    total = QUAD * rows
    ups = max(depth - 2, 1)
    dma = pltpu.SemaphoreType.DMA
    any_spec = pl.BlockSpec(memory_space=pl.ANY)
    hbm_spec = pl.BlockSpec(memory_space=pltpu.HBM)
    vmem_spec = pl.BlockSpec(memory_space=pltpu.VMEM)
    like = jax.ShapeDtypeStruct((rows, width), BF16)
    out = pl.pallas_call(
        functools.partial(kernel, seq_count, rows, own_heads),
        out_shape=(like, like, like, like, jax.ShapeDtypeStruct((2, DH), F32)),
        in_specs=[hbm_spec] * 6,
        out_specs=(any_spec,) * 4 + (vmem_spec,),
        scratch_shapes=[
            pltpu.VMEM((4, own_heads, total, DH), BF16),
            pltpu.VMEM((4, own_heads, total, DH), BF16),
            pltpu.VMEM((own_heads, 2 * total, DH), BF16),
            pltpu.VMEM((own_heads, 2, 2 * total, DH), BF16),
            pltpu.VMEM((own_heads, ups, 2, rows, DH), BF16),
            pltpu.VMEM((own_heads, ups, 2, rows, DH), BF16),
            pltpu.VMEM((own_heads, ups, 2, rows, DH), BF16),
            pltpu.VMEM((total, DH), F32),
            pltpu.VMEM((2 * total, DH), F32),
            pltpu.VMEM((2 * total, DH), F32),
            pltpu.VMEM((own_heads, 2 * total, DH), F32),
            pltpu.VMEM((own_heads, 2 * total, DH), F32),
            pltpu.VMEM((own_heads, 2 * total, DH), F32),
            pltpu.VMEM((2 * total, DH), F32),
            pltpu.VMEM((2 * total, DH), F32),
            pltpu.VMEM((own_heads, total, 2 * rows), BF16),
            pltpu.VMEM((own_heads, 2, rows, rows), BF16),
            pltpu.VMEM((ups, rows, rows), BF16),
            pltpu.VMEM((2, 1, DH), F32),
            pltpu.VMEM((8, DH), F32),
            pltpu.VMEM((2, 8, DH), F32),
            pltpu.VMEM((QUAD, 8, DH), F32),
            pltpu.VMEM((groups, 8, DH), F32),
            pltpu.VMEM((1, 8, DH), F32),
            pltpu.VMEM((2, own_heads, total, DH), F32),
        ]
        + [dma((4, own_heads, QUAD))] * 4
        + [dma((own_heads, groups))] * 4
        + [dma((QUAD,))] * 2
        + [dma((groups,))] * 2
        + [dma((1,))] * 2
        + [dma((2,)), pltpu.SemaphoreType.REGULAR],
        compiler_params=pltpu.CompilerParams(
            collective_id=0, has_side_effects=True, vmem_limit_bytes=48 << 20
        ),
    )(
        *(
            pltpu.with_memory_space_constraint(x, pltpu.HBM)
            for x in (
                queries, key_vectors, value_vectors, grad_out,
                gain_query.reshape(1, DH), gain_key.reshape(1, DH),
            )
        )
    )
    return pl.pallas_call(
        store_kernel,
        out_shape=(like, like, like, like, jax.ShapeDtypeStruct((2, DH), F32)),
        in_specs=[any_spec] * 4 + [vmem_spec],
        out_specs=(hbm_spec,) * 4 + (vmem_spec,),
        scratch_shapes=[dma((4,))],
        compiler_params=pltpu.CompilerParams(vmem_limit_bytes=4 << 20),
    )(*out)


def solution(mesh):
    in_specs = (P("seq", "head"), P("seq", "head"), P("seq", "head"), P(), P(), P("seq", "head"))
    out_specs = (P("seq", "head"), P("seq", "head"), P("seq", "head"), P("seq", "head"), P())
    return jax.shard_map(
        per_device, mesh=mesh, in_specs=in_specs, out_specs=out_specs, check_vma=False
    )
```
